32 devices in a mesh: dp: 8 (over z, y), fsdp: 4 (over x, core).
Axes of the slice: x: 2, y: 2, z: 4, core: 2. Of those that a mesh axis runs over, the one named last changes fastest.
Arguments:
- byte_tokens: int32 [4096, 8], P(('dp', 'fsdp')), may hold values from 0 to 255
- byte_mask: int32 [4096, 8], P(('dp', 'fsdp')), may hold values from 0 to 1, as said below
- patch_item: int32 [4096], P(('dp', 'fsdp')), may hold values from 0 to 2, as said below
- cotangent: bfloat16 [32768, 768], P(('dp', 'fsdp')), may hold values from -16 to 16
- embed: float32 [256, 768], P('dp', 'fsdp'), may hold values from -6 to 6
- patch_weight: float32 [6144, 768], P('dp', 'fsdp'), may hold values from -0.078125 to 0.078125
- gain_attn: float32 [768], P(('dp', 'fsdp')), may hold values from 0.5 to 1.5
- qkv_weight: float32 [768, 2304], P('dp', 'fsdp'), may hold values from -0.21875 to 0.21875
- out_weight: float32 [768, 768], P('dp', 'fsdp'), may hold values from -0.625 to 0.625
- gain_mlp: float32 [768], P(('dp', 'fsdp')), may hold values from 0.5 to 1.5
- up_weight: float32 [768, 3072], P('dp', 'fsdp'), may hold values from -0.21875 to 0.21875
- down_weight: float32 [3072, 768], P('dp', 'fsdp'), may hold values from -0.109375 to 0.109375
- global_to_local: float32 [768, 6144], P('dp', 'fsdp'), may hold values from -0.21875 to 0.21875
- gain_local: float32 [768], P(('dp', 'fsdp')), may hold values from 0.5 to 1.5
- local_up: float32 [768, 3072], P('dp', 'fsdp'), may hold values from -0.21875 to 0.21875
- local_down: float32 [3072, 768], P('dp', 'fsdp'), may hold values from -0.109375 to 0.109375
Outputs:
- byte_out: bfloat16 [32768, 768], P(('dp', 'fsdp'))
- embed_grad: float32 [256, 768], P('dp', 'fsdp')
- patch_grad: float32 [6144, 768], P('dp', 'fsdp')
- gain_attn_grad: float32 [768], P(('dp', 'fsdp'))
- qkv_grad: float32 [768, 2304], P('dp', 'fsdp')
- out_grad: float32 [768, 768], P('dp', 'fsdp')
- gain_mlp_grad: float32 [768], P(('dp', 'fsdp'))
- up_grad: float32 [768, 3072], P('dp', 'fsdp')
- down_grad: float32 [3072, 768], P('dp', 'fsdp')
- link_grad: float32 [768, 6144], P('dp', 'fsdp')
- gain_local_grad: float32 [768], P(('dp', 'fsdp'))
- local_up_grad: float32 [768, 3072], P('dp', 'fsdp')
- local_down_grad: float32 [3072, 768], P('dp', 'fsdp')
The draws below stay inside these ranges and needn't reach their ends.
Inputs may be any that keep to these rules, and one draw needn't show every extreme that they name: `patch_item`: within each block of 128 patches the values start at 0 and never fall; 0 and 1 are two whole items, each of one patch or more; 2 marks padding patches after them, with no live bytes. The items of a block cover from 80 to 128 patches, both reached in every draw. `byte_mask`: every patch of an item has all 8 bytes live except the item's last patch, which has 1 to 8 live bytes at its start.
All inputs are finite; a program needn't handle non-finite values.
Results may differ from the reference program's by a relative error of at most 0.024.
Values may be sent and summed in bfloat16 or wider, within the bound.
No kernel may reach another device: no remote copies, remote signals or barrier semaphores. Data moves between devices by JAX's collectives and lax.ppermute only.
A program may use at most 192 MiB of HBM per device.

```python
import jax
import jax.numpy as jnp
from jax import lax

D = 768
HEADS = 12
HEAD_DIM = 64
FF = 3072
VOCAB = 256
PATCH = 8
PATCH_DEV = 128
PATCHES = 4096
PD = 6144
N_DP = 8
N_FSDP = 4


def layout(key):
    blocks = PATCHES // PATCH_DEV
    live = jax.random.randint(jax.random.fold_in(key, 11), (blocks,), PATCH_DEV * 5 // 8, PATCH_DEV + 1)
    live = live.at[0].set(PATCH_DEV).at[1].set(PATCH_DEV * 5 // 8)
    fraction = jax.random.randint(jax.random.fold_in(key, 12), (blocks,), 0, 1 << 20)
    cutting = 1 + fraction * (live - 1) // (1 << 20)
    tails = jax.random.randint(jax.random.fold_in(key, 13), (blocks, 2), 1, PATCH + 1)
    tails = tails.at[0, 0].set(1).at[0, 1].set(PATCH)
    place = jnp.arange(PATCH_DEV)[None, :]
    items = (place >= cutting[:, None]).astype(jnp.int32) + (place >= live[:, None]).astype(jnp.int32)
    first_last = place == cutting[:, None] - 1
    second_last = place == live[:, None] - 1
    counted = jnp.where(first_last, tails[:, 0:1], jnp.where(second_last, tails[:, 1:2], jnp.where(items < 2, PATCH, 0)))
    lanes = jnp.arange(PATCH)
    masked = (lanes[None, None, :] < counted[:, :, None]).astype(jnp.int32)
    return (items.reshape(PATCHES), masked.reshape(PATCHES, PATCH))


def draw_patch_item(key, part):
    return layout(key)[0]


def draw_byte_mask(key, part):
    return layout(key)[1]


def draw_cotangent(key, part):
    total_rows = PATCHES * PATCH
    blocks = PATCHES // PATCH_DEV
    device = jnp.arange(total_rows) // (PATCH_DEV * PATCH)
    position = device.astype(jnp.float32) / max(blocks - 1, 1)
    base = jnp.clip(jax.random.normal(key, (total_rows, D), jnp.float32), -5.0, 5.0)
    factor = 1.0 + 2.0 * position
    return (base * factor[:, None]).astype(jnp.bfloat16)


def with_ends(values, key, low, top_value):
    longest = values.shape.index(max(values.shape))
    spots = []
    for shift in (0, 1):
        where = [jax.random.randint(jax.random.fold_in(key, axis), (), 0, length) for axis, length in enumerate(values.shape)]
        where[longest] = (where[longest] + shift) % values.shape[longest]
        spots.append(tuple(where))
    return values.at[spots[0]].set(low).at[spots[1]].set(top_value)


def block_scale(rng, extent, split, smallest, top_value):
    level = 1.0
    for axis_at, shards_of in split:
        steps = jax.random.uniform(jax.random.fold_in(jax.random.fold_in(rng, 6), axis_at), (shards_of,), jnp.float32, smallest / len(split), top_value / len(split))
        level = level * jnp.repeat(jnp.exp(steps), extent[axis_at] // shards_of).reshape((-1,) + (1,) * (len(extent) - 1 - axis_at))
    return level


def gaussian(rng, dims, scale, limit, shards=(), kind=jnp.bfloat16):
    loudness = block_scale(rng, dims, shards, -0.22, 0.18) if shards else 1.0
    entries = jax.random.normal(rng, dims, jnp.float32) * scale * loudness
    return jnp.minimum(jnp.maximum(entries, -limit), limit).astype(kind)


def setup_inputs(seed: int = 0) -> dict:
    key_of = jax.random.split(jax.random.key(seed), 17)
    return {
        "byte_tokens": with_ends(jax.random.randint(key_of[0], (PATCHES, PATCH), 0, VOCAB), jax.random.fold_in(key_of[0], 1), 0, VOCAB - 1).astype(jnp.int32),
        "byte_mask": draw_byte_mask(jax.random.fold_in(key_of[16], 71), 0),
        "patch_item": draw_patch_item(jax.random.fold_in(key_of[16], 71), 0),
        "cotangent": draw_cotangent(jax.random.fold_in(key_of[16], 71), 0),
        "embed": gaussian(key_of[4], (VOCAB, D), 1.0, 6.0, ((0, 8), (1, 4)), jnp.float32),
        "patch_weight": gaussian(key_of[5], (PD, D), PD ** -0.5, 0.078125, ((0, 8), (1, 4)), jnp.float32),
        "gain_attn": jnp.clip(1.0 + 0.1 * jax.random.normal(key_of[6], (D,), jnp.float32), 0.5, 1.5),
        "qkv_weight": gaussian(key_of[7], (D, 3 * D), D ** -0.5, 0.21875, ((0, 8), (1, 4)), jnp.float32),
        "out_weight": gaussian(key_of[8], (D, D), (D // 8) ** -0.5, 0.625, ((0, 8), (1, 4)), jnp.float32),
        "gain_mlp": jnp.clip(1.0 + 0.1 * jax.random.normal(key_of[9], (D,), jnp.float32), 0.5, 1.5),
        "up_weight": gaussian(key_of[10], (D, FF), D ** -0.5, 0.21875, ((0, 8), (1, 4)), jnp.float32),
        "down_weight": gaussian(key_of[11], (FF, D), FF ** -0.5, 0.109375, ((0, 8), (1, 4)), jnp.float32),
        "global_to_local": gaussian(key_of[12], (D, PD), D ** -0.5, 0.21875, ((0, 8), (1, 4)), jnp.float32),
        "gain_local": jnp.clip(1.0 + 0.1 * jax.random.normal(key_of[13], (D,), jnp.float32), 0.5, 1.5),
        "local_up": gaussian(key_of[14], (D, FF), D ** -0.5, 0.21875, ((0, 8), (1, 4)), jnp.float32),
        "local_down": gaussian(key_of[15], (FF, D), FF ** -0.5, 0.109375, ((0, 8), (1, 4)), jnp.float32),
    }


EPS = 1e-05

@jax.custom_vjp
def low(v):
    return lax.optimization_barrier(v.astype(jnp.bfloat16)).astype(jnp.float32)

@jax.custom_vjp
def low_back(v):
    return v

def low_keep(v):
    return (low(v), None)

def low_pass(kept, grad):
    return (grad,)

def back_keep(v):
    return (v, None)

def back_low(kept, grad):
    return (low(grad),)
low.defvjp(low_keep, low_pass)
low_back.defvjp(back_keep, back_low)

def rounded(value):
    return low(low_back(value))

def matmul(left, right):
    return jnp.dot(left, right, precision=lax.Precision.HIGHEST, preferred_element_type=jnp.float32)

def layer_norm(value, gain):
    center = value - lax.optimization_barrier(jnp.mean(value, axis=-1, keepdims=True))
    spread = lax.optimization_barrier(jnp.mean(center * center, axis=-1, keepdims=True))
    return center * lax.rsqrt(spread + EPS) * gain

def device_block(weights, tokens, mask, items):
    w_embed, w_patch, gain_attn, w_qkv, w_out, gain_mlp, w_up, w_down, w_link, gain_local, w_local_up, w_local_down = weights
    onehot = (tokens.reshape(-1)[:, None] == jnp.arange(VOCAB)[None, :]).astype(jnp.float32)
    byte_live = mask.reshape(-1).astype(jnp.float32)[:, None]
    byte_emb = low_back(matmul(onehot, w_embed) * byte_live)
    patch_in = byte_emb.reshape(PATCH_DEV, PATCH * D)
    patch_emb = low_back(matmul(patch_in, w_patch))
    same_item = (items[1:] == items[:-1]).astype(jnp.float32)[:, None]
    global_in = jnp.concatenate([jnp.zeros((1, D), jnp.float32), patch_emb[:-1] * same_item], axis=0)
    normed_attn = low(layer_norm(global_in, gain_attn))
    qkv_rows = rounded(matmul(normed_attn, w_qkv))
    parts = qkv_rows.reshape(PATCH_DEV, 3, HEADS, HEAD_DIM)
    raw = jnp.einsum('qhd,khd->hqk', parts[:, 0], parts[:, 1], precision=lax.Precision.HIGHEST)
    scores = low_back(raw * HEAD_DIM ** (-0.5))
    places = jnp.arange(PATCH_DEV)
    allowed = (items[:, None] == items[None, :]) & (places[:, None] >= places[None, :])
    probs = low(jax.nn.softmax(jnp.where(allowed[None], scores, -jnp.inf), axis=-1))
    mixed = jnp.einsum('hqk,khd->qhd', probs, parts[:, 2], precision=lax.Precision.HIGHEST)
    mixed = rounded(mixed.reshape(PATCH_DEV, D))
    after_attn = global_in + low_back(matmul(mixed, w_out))
    normed_mlp = low(layer_norm(after_attn, gain_mlp))
    hidden_act = low(jax.nn.gelu(low_back(matmul(normed_mlp, w_up))))
    global_out = after_attn + low_back(matmul(hidden_act, w_down))
    from_global = low_back(matmul(low(global_out), w_link)).reshape(PATCH_DEV * PATCH, D)
    grouped = byte_emb.reshape(PATCH_DEV, PATCH, D)
    prev_emb = jnp.concatenate([jnp.zeros((PATCH_DEV, 1, D), jnp.float32), grouped[:, :-1]], axis=1)
    local_in = from_global + prev_emb.reshape(PATCH_DEV * PATCH, D)
    normed_local = low(layer_norm(local_in, gain_local))
    local_act = low(jax.nn.gelu(low_back(matmul(normed_local, w_local_up))))
    local_out = local_in + low_back(matmul(local_act, w_local_down))
    return local_out * byte_live

def reference(byte_tokens, byte_mask, patch_item, cotangent, embed, patch_weight, gain_attn, qkv_weight, out_weight, gain_mlp, up_weight, down_weight, global_to_local, gain_local, local_up, local_down):
    devices_all = N_DP * N_FSDP
    tokens = byte_tokens.reshape(devices_all, PATCH_DEV, PATCH)
    masks = byte_mask.reshape(devices_all, PATCH_DEV, PATCH)
    items = patch_item.reshape(devices_all, PATCH_DEV)
    masters = (embed, patch_weight, gain_attn, qkv_weight, out_weight, gain_mlp, up_weight, down_weight, global_to_local, gain_local, local_up, local_down)
    block_step = jax.checkpoint(device_block)

    def forward(weights):
        lowered = tuple((low(weight) for weight in weights))

        def one_device(inputs):
            return block_step(lowered, inputs[0], inputs[1], inputs[2])
        return lax.map(one_device, (tokens, masks, items)).reshape(PATCHES * PATCH, D)
    result, pull = jax.vjp(forward, masters)
    grads = pull(cotangent.astype(jnp.float32))[0]
    return (result.astype(jnp.bfloat16), grads[0], grads[1], grads[2], grads[3], grads[4], grads[5], grads[6], grads[7], grads[8], grads[9], grads[10], grads[11])
```

```python
import jax
import jax.numpy as jnp
from jax import lax
from jax.sharding import PartitionSpec as P

HEADS = 12
HEAD_DIM = 64
EPS = 1e-05
LOW = jnp.bfloat16


def over_rows(left, right):
    return lax.dot_general(
        left, right, (((0,), (0,)), ((), ())), preferred_element_type=jnp.float32
    )


def times_back(left, right):
    return lax.dot_general(
        left, right, (((1,), (1,)), ((), ())), preferred_element_type=jnp.float32
    )


def matmul(left, right):
    return jnp.dot(left, right, preferred_element_type=jnp.float32)


def norm_rows(value, gain):
    center = value - jnp.mean(value, axis=-1, keepdims=True)
    spread = jnp.mean(center * center, axis=-1, keepdims=True)
    return center * lax.rsqrt(spread + EPS) * gain


def norm_back(value, gain, grad):
    unused, pull = jax.vjp(norm_rows, value, gain.astype(jnp.float32))
    return pull(grad)


def gelu_back(value, grad):
    unused, pull = jax.vjp(jax.nn.gelu, value)
    return pull(grad)[0]


def split_heads(qkv_rows):
    parts = qkv_rows.reshape(qkv_rows.shape[0], 3, HEADS, HEAD_DIM)
    return (parts[:, 0], parts[:, 1], parts[:, 2])


def score_rows(queries, keys, items):
    raw = jnp.einsum(
        "qhd,khd->hqk", queries, keys, preferred_element_type=jnp.float32
    ) * HEAD_DIM ** (-0.5)
    places = jnp.arange(items.shape[0])
    allowed = (items[:, None] == items[None, :]) & (places[:, None] >= places[None, :])
    return jnp.where(allowed[None], raw, -jnp.inf)


def attend(qkv_rows, items):
    queries, keys, values = split_heads(qkv_rows)
    masked = score_rows(queries, keys, items)
    peak = jnp.max(masked, axis=-1, keepdims=True)
    log_total = peak + jnp.log(jnp.sum(jnp.exp(masked - peak), axis=-1, keepdims=True))
    probs = jnp.exp(masked - log_total).astype(LOW)
    mixed = jnp.einsum("hqk,khd->qhd", probs, values, preferred_element_type=jnp.float32)
    return (mixed.reshape(qkv_rows.shape[0], HEADS * HEAD_DIM).astype(LOW), log_total)


def attend_back(qkv_rows, items, log_total, grad_mixed):
    queries, keys, values = split_heads(qkv_rows)
    count = qkv_rows.shape[0]
    probs = jnp.exp(score_rows(queries, keys, items) - log_total)
    grad_heads = grad_mixed.reshape(count, HEADS, HEAD_DIM)
    grad_probs = jnp.einsum("qhd,khd->hqk", grad_heads, values, preferred_element_type=jnp.float32)
    delta = jnp.sum(probs * grad_probs, axis=-1, keepdims=True)
    grad_scores = (probs * (grad_probs - delta)).astype(LOW)
    scale = HEAD_DIM ** (-0.5)
    grad_q = (
        jnp.einsum("hqk,khd->qhd", grad_scores, keys, preferred_element_type=jnp.float32) * scale
    )
    grad_k = (
        jnp.einsum("hqk,qhd->khd", grad_scores, queries, preferred_element_type=jnp.float32) * scale
    )
    grad_v = jnp.einsum(
        "hqk,qhd->khd", probs.astype(LOW), grad_heads, preferred_element_type=jnp.float32
    )
    return (
        jnp.stack([grad_q, grad_k, grad_v], axis=1)
        .reshape(count, 3 * HEADS * HEAD_DIM)
        .astype(LOW)
    )


class Links:
    def __init__(self, n_dp, n_fsdp):
        self.n, self.m = n_dp, n_fsdp
        self.hi = n_fsdp // 2
        self.order = [0, 2, 4, 6, 7, 5, 3, 1] if n_dp == 8 else list(range(n_dp))
        self.d = lax.axis_index("dp")
        self.f = lax.axis_index("fsdp")
        self.core = self.f % 2
        place = [self.order.index(i) for i in range(n_dp)]
        spot = jnp.array(place, jnp.int32)[self.d]
        table = jnp.array(self.order, jnp.int32)
        self.at = {k: table[(spot + k) % n_dp] for k in range(1 - n_dp, n_dp)}

    def shift(self, value, step):
        n, order = self.n, self.order
        return lax.ppermute(value, "dp", [(order[i], order[(i + step) % n]) for i in range(n)])

    def swap(self, value, bit, axis="fsdp"):
        size = self.m if axis == "fsdp" else self.n
        return lax.ppermute(value, axis, [(i, i ^ bit) for i in range(size)])

    def bits(self, size, low=1):
        found, bit = [], low
        while bit < size:
            found.append(bit)
            bit *= 2
        return found

    def ring_gather(self, piece, flip):
        n = self.n
        far = n // 2
        forward, backward = (far, n - 1 - far) if flip else (n - 1 - far, far)
        whole = jnp.zeros((n,) + piece.shape, piece.dtype)
        whole = lax.dynamic_update_slice(whole, piece[None], (self.d, 0, 0))
        right = left = piece
        for step in range(1, far + 1):
            if step <= forward:
                right = self.shift(right, 1)
                whole = lax.dynamic_update_slice(whole, right[None], (self.at[-step], 0, 0))
            if step <= backward:
                left = self.shift(left, -1)
                whole = lax.dynamic_update_slice(whole, left[None], (self.at[step], 0, 0))
        return whole.reshape(n * piece.shape[0], piece.shape[1])

    def ring_scatter(self, total, flip):
        n = self.n
        rows = total.shape[0] // n
        far = n // 2
        forward, backward = (far, n - 1 - far) if flip else (n - 1 - far, far)

        def mine(k):
            return lax.dynamic_slice_in_dim(total, self.at[k] * rows if k else self.d * rows, rows, 0)

        right = left = None
        for step in range(far, 0, -1):
            if step <= forward:
                part = mine(step)
                if right is not None:
                    part = (part.astype(jnp.float32) + right.astype(jnp.float32)).astype(LOW)
                right = self.shift(part, 1)
            if step <= backward:
                part = mine(-step)
                if left is not None:
                    part = (part.astype(jnp.float32) + left.astype(jnp.float32)).astype(LOW)
                left = self.shift(part, -1)
        return mine(0).astype(jnp.float32) + right.astype(jnp.float32) + left.astype(jnp.float32)

    def pair_columns(self, value):
        rows, columns = value.shape
        parts = value.reshape(rows, self.hi, 2, columns // self.m)
        return parts.transpose(0, 2, 1, 3).reshape(rows, columns)

    def unpair_columns(self, value):
        rows, columns = value.shape
        parts = value.reshape(rows, 2, self.hi, columns // self.m)
        return parts.transpose(0, 2, 1, 3).reshape(rows, columns)

    def gather_hi(self, piece):
        group = piece[None]
        for bit in self.bits(self.m, 2):
            other = self.swap(group, bit)
            group = jnp.where(
                (self.f & bit) != 0,
                jnp.concatenate([other, group]),
                jnp.concatenate([group, other]),
            )
        return group.transpose(1, 0, 2).reshape(piece.shape[0], -1)

    def gather_paired(self, piece, flip):
        slab = self.ring_gather(piece, flip)
        other = self.swap(slab, 1)
        width = slab.shape[1]
        whole = jnp.zeros((slab.shape[0], 2 * width), slab.dtype)
        whole = lax.dynamic_update_slice(whole, slab, (0, self.core * width))
        return lax.dynamic_update_slice(whole, other, (0, (1 - self.core) * width))

    def gather_slabs(self, piece, flip):
        slabs = {0: self.ring_gather(piece, flip)}
        for bit in reversed(self.bits(self.m)):
            slabs.update({q ^ bit: self.swap(slab, bit) for q, slab in list(slabs.items())})
        rows, width = slabs[0].shape
        whole = jnp.zeros((rows, self.m * width), piece.dtype)
        for q, slab in slabs.items():
            whole = lax.dynamic_update_slice(whole, slab, (0, (self.f ^ q) * width))
        return whole

    def half(self, value, which):
        width = value.shape[1] // 2
        return lax.dynamic_slice_in_dim(value, which * width, width, 1)

    def scatter_paired(self, left, right_paired):
        sent = over_rows(left, self.half(right_paired, 1 - self.core)).astype(LOW)
        got = self.swap(sent, 1)
        kept = over_rows(left, self.half(right_paired, self.core))
        return (kept + got.astype(jnp.float32)).astype(LOW)

    def scatter_hi(self, total):
        rows = total.shape[0]
        group = total.reshape(rows, self.hi, -1).transpose(1, 0, 2)
        for bit in reversed(self.bits(self.m, 2)):
            keep, give = jnp.split(group, 2)
            high = (self.f & bit) != 0
            keep, give = jnp.where(high, give, keep), jnp.where(high, keep, give)
            group = keep + self.swap(give.astype(LOW), bit).astype(jnp.float32)
        return group[0]

    def scatter_slabs(self, left, right):
        width = right.shape[1] // self.m

        def slab(q):
            part = lax.dynamic_slice_in_dim(right, (self.f ^ q) * width, width, 1)
            return over_rows(left, part)

        sums = {}
        for q in reversed(range(0, self.m, 2)):
            got = self.swap(slab(q ^ 1).astype(LOW), 1)
            sums[q] = slab(q) + got.astype(jnp.float32)
        for bit in self.bits(self.m, 2):
            step = {}
            for q in sums:
                if not q & bit:
                    got = self.swap(sums[q ^ bit].astype(LOW), bit)
                    step[q] = sums[q] + got.astype(jnp.float32)
            sums = step
        return sums[0].astype(LOW)

    def gather_all(self, piece):
        group = piece[None]
        steps = [("dp", bit) for bit in reversed(self.bits(self.n))]
        steps += [("fsdp", bit) for bit in reversed(self.bits(self.m))]
        for axis, bit in steps:
            index = self.d if axis == "dp" else self.f
            other = self.swap(group, bit, axis)
            pair = jnp.where(
                (index & bit) != 0, jnp.stack([other, group]), jnp.stack([group, other])
            )
            group = pair.reshape((-1,) + piece.shape)
        count = len(steps)
        group = group.reshape((2,) * count + piece.shape)
        order = tuple(reversed(range(count))) + (count, count + 1)
        return group.transpose(order).reshape((self.n, self.m) + piece.shape)

    def scatter_all(self, total):
        steps = [("fsdp", bit) for bit in self.bits(self.m)]
        steps += [("dp", bit) for bit in self.bits(self.n)]
        count = len(steps)
        tail = total.shape[2:]
        group = total.reshape((2,) * count + tail)
        log_n = len(self.bits(self.n))
        order = tuple(range(log_n, count))[::-1] + tuple(range(log_n))[::-1]
        group = group.transpose(order + (count, count + 1))
        for axis, bit in steps:
            index = self.d if axis == "dp" else self.f
            high = (index & bit) != 0
            keep = jnp.where(high, group[1], group[0])
            give = jnp.where(high, group[0], group[1])
            group = keep + self.swap(give.astype(LOW), bit, axis).astype(jnp.float32)
        return group


def per_device(
    n_dp,
    n_fsdp,
    byte_tokens,
    byte_mask,
    patch_item,
    cotangent,
    embed,
    patch_weight,
    gain_attn,
    qkv_weight,
    out_weight,
    gain_mlp,
    up_weight,
    down_weight,
    global_to_local,
    gain_local,
    local_up,
    local_down,
):
    links = Links(n_dp, n_fsdp)
    npatch, patch_len = byte_tokens.shape
    nbyte = npatch * patch_len
    vocab = embed.shape[0] * n_dp
    width = embed.shape[1] * n_fsdp
    low_patch = patch_weight.astype(LOW)

    gains = jnp.stack([gain_attn, gain_mlp, gain_local]).astype(LOW)
    per_gain = gains.shape[1]
    small = jnp.zeros((embed.shape[0] + 16, embed.shape[1]), LOW)
    small = small.at[: embed.shape[0]].set(embed.astype(LOW))
    small = small.at[embed.shape[0], : 3 * per_gain].set(gains.reshape(-1))
    everyone = links.gather_all(small)
    w_embed = everyone[:, :, : embed.shape[0]].transpose(0, 2, 1, 3).reshape(vocab, width)
    all_gains = everyone[:, :, embed.shape[0], : 3 * per_gain].reshape(-1, 3, per_gain)
    all_gains = all_gains.transpose(1, 0, 2).reshape(3, width).astype(jnp.float32)
    g_attn, g_mlp, g_local = all_gains[0], all_gains[1], all_gains[2]

    rows = patch_weight.shape[0]
    per_place = n_dp // patch_len
    part = (links.d % per_place) * rows
    embed_part = lax.dynamic_slice_in_dim(w_embed, part, rows, 1)
    table = matmul(embed_part, low_patch).astype(LOW)

    qkv_pair = links.gather_hi(qkv_weight.astype(LOW))
    out_pair = links.gather_hi(out_weight.astype(LOW))
    down_pair = links.gather_hi(down_weight.astype(LOW))
    local_down_pair = links.gather_hi(local_down.astype(LOW))
    table_pair = links.gather_hi(table)

    w_table = links.gather_paired(table_pair, True)
    w_qkv = links.gather_paired(qkv_pair, False)
    w_out = links.gather_paired(out_pair, True)
    w_up = links.gather_slabs(up_weight.astype(LOW), True)
    w_down = links.gather_paired(down_pair, False)
    w_link = links.gather_slabs(global_to_local.astype(LOW), True)
    w_local_up = links.gather_slabs(local_up.astype(LOW), False)
    w_local_down = links.gather_paired(local_down_pair, True)

    byte_live = byte_mask.reshape(-1).astype(jnp.float32)[:, None]
    marked = jnp.where(byte_mask != 0, byte_tokens, -1)
    before = jnp.concatenate([jnp.full((npatch, 1), -1, jnp.int32), marked[:, :-1]], axis=1)
    values = jnp.arange(vocab, dtype=jnp.int32)
    hot_before = (before.reshape(-1)[:, None] == values[None, :]).astype(LOW)
    hot_patch = jnp.repeat(marked, per_place, axis=1)[:, :, None] == values[None, None, :]
    hot_patch = hot_patch.astype(LOW).reshape(npatch, n_dp * vocab)
    grad_out = cotangent.astype(jnp.float32) * byte_live
    grad_lout = links.pair_columns(grad_out.astype(LOW))

    patch_emb = links.unpair_columns(matmul(hot_patch, w_table))
    same_item = (patch_item[1:] == patch_item[:-1]).astype(jnp.float32)[:, None]
    global_in = jnp.concatenate(
        [jnp.zeros((1, width), jnp.float32), patch_emb[:-1] * same_item], axis=0
    )
    normed_attn = norm_rows(global_in, g_attn).astype(LOW)
    qkv_rows = links.unpair_columns(matmul(normed_attn, w_qkv).astype(LOW))
    mixed, log_total = attend(qkv_rows, patch_item)
    after_attn = global_in + links.unpair_columns(matmul(mixed, w_out))
    normed_mlp = norm_rows(after_attn, g_mlp).astype(LOW)
    hidden_pre = matmul(normed_mlp, w_up)
    hidden_act = jax.nn.gelu(hidden_pre).astype(LOW)
    global_out = after_attn + links.unpair_columns(matmul(hidden_act, w_down))
    global_low = global_out.astype(LOW)
    from_global = matmul(global_low, w_link).reshape(nbyte, width)
    local_in = from_global + matmul(hot_before, w_embed)
    normed_local = norm_rows(local_in, g_local).astype(LOW)
    local_pre = matmul(normed_local, w_local_up)
    local_act = jax.nn.gelu(local_pre).astype(LOW)
    local_out = local_in + links.unpair_columns(matmul(local_act, w_local_down))
    result = (local_out * byte_live).astype(LOW)

    down_sum = links.ring_scatter(links.scatter_paired(local_act, grad_lout), True)
    local_down_grad = links.scatter_hi(down_sum)
    grad_local_act = times_back(grad_lout, w_local_down)
    grad_local_pre = gelu_back(local_pre, grad_local_act).astype(LOW)
    local_up_grad = links.ring_scatter(links.scatter_slabs(normed_local, grad_local_pre), False)
    grad_normed_local = times_back(grad_local_pre, w_local_up)
    grad_local_in, grad_gain_local = norm_back(local_in, g_local, grad_normed_local)
    grad_local_in = grad_local_in + grad_out
    grad_local_low = grad_local_in.astype(LOW)
    grad_link_in = grad_local_low.reshape(npatch, patch_len * width)
    link_grad = links.ring_scatter(links.scatter_slabs(global_low, grad_link_in), True)
    grad_global_out = times_back(grad_link_in, w_link)
    embed_direct = over_rows(hot_before, grad_local_low)

    grad_mlp = grad_global_out.astype(LOW)
    grad_mlp_paired = links.pair_columns(grad_mlp)
    down_grad = links.scatter_hi(
        links.ring_scatter(links.scatter_paired(hidden_act, grad_mlp_paired), False)
    )
    grad_hidden = times_back(grad_mlp_paired, w_down)
    grad_hidden_pre = gelu_back(hidden_pre, grad_hidden).astype(LOW)
    up_grad = links.ring_scatter(links.scatter_slabs(normed_mlp, grad_hidden_pre), True)
    grad_normed_mlp = times_back(grad_hidden_pre, w_up)
    grad_after, grad_gain_mlp = norm_back(after_attn, g_mlp, grad_normed_mlp)
    grad_after = grad_after + grad_global_out
    grad_attn = links.pair_columns(grad_after.astype(LOW))
    out_grad = links.scatter_hi(
        links.ring_scatter(links.scatter_paired(mixed, grad_attn), False)
    )
    grad_mixed = times_back(grad_attn, w_out).astype(LOW)
    grad_qkv = links.pair_columns(attend_back(qkv_rows, patch_item, log_total, grad_mixed))
    qkv_grad = links.scatter_hi(
        links.ring_scatter(links.scatter_paired(normed_attn, grad_qkv), True)
    )
    grad_normed_attn = times_back(grad_qkv, w_qkv)
    grad_global_in, grad_gain_attn = norm_back(global_in, g_attn, grad_normed_attn)
    grad_global_in = grad_global_in + grad_after
    grad_patch_emb = jnp.concatenate(
        [grad_global_in[1:] * same_item, jnp.zeros((1, width), jnp.float32)], axis=0
    ).astype(LOW)
    table_grad = links.scatter_hi(
        links.ring_scatter(
            links.scatter_paired(hot_patch, links.pair_columns(grad_patch_emb)), False
        )
    ).astype(LOW)
    patch_grad = over_rows(embed_part, table_grad)
    embed_partial = lax.dynamic_update_slice(
        jnp.zeros((vocab, width), jnp.float32), times_back(table_grad, low_patch), (0, part)
    )
    embed_partial = (embed_partial + embed_direct).reshape(n_dp, -1, n_fsdp, embed.shape[1])
    gain_grads = jnp.stack([grad_gain_attn, grad_gain_mlp, grad_gain_local])
    gain_grads = gain_grads.reshape(3, n_dp, n_fsdp, per_gain).transpose(1, 2, 0, 3)
    packed = jnp.zeros((n_dp, n_fsdp) + small.shape, jnp.float32)
    packed = packed.at[:, :, : embed.shape[0]].set(embed_partial.transpose(0, 2, 1, 3))
    packed = packed.at[:, :, embed.shape[0], : 3 * per_gain].set(
        gain_grads.reshape(n_dp, n_fsdp, 3 * per_gain)
    )
    sums = links.scatter_all(packed)
    embed_grad = sums[: embed.shape[0]]
    gain_sums = sums[embed.shape[0], : 3 * per_gain].reshape(3, per_gain)
    return (
        result,
        embed_grad,
        patch_grad,
        gain_sums[0],
        qkv_grad,
        out_grad,
        gain_sums[1],
        up_grad,
        down_grad,
        link_grad,
        gain_sums[2],
        local_up_grad,
        local_down_grad,
    )


def solution(mesh):
    n_dp, n_fsdp = mesh.shape["dp"], mesh.shape["fsdp"]

    def body(*args):
        return per_device(n_dp, n_fsdp, *args)

    items = P(("dp", "fsdp"), None)
    weight = P("dp", "fsdp")
    flat = P(("dp", "fsdp"))
    weights = (weight, weight, flat, weight, weight, flat, weight, weight, weight, flat, weight, weight)
    return jax.shard_map(
        body,
        mesh=mesh,
        in_specs=(items, items, flat, items) + weights,
        out_specs=(items,) + weights,
        check_vma=False,
    )
```

```python
import jax
import jax.numpy as jnp
from jax import lax
from jax.experimental import pallas as pl
from jax.experimental.pallas import tpu as pltpu
from jax.sharding import PartitionSpec as P

HEADS = 12
HEAD_DIM = 64
EPS = 1e-05
LOW = jnp.bfloat16


def over_rows(left, right):
    return lax.dot_general(
        left, right, (((0,), (0,)), ((), ())), preferred_element_type=jnp.float32
    )


def times_back(left, right):
    return lax.dot_general(
        left, right, (((1,), (1,)), ((), ())), preferred_element_type=jnp.float32
    )


def matmul(left, right):
    return jnp.dot(left, right, preferred_element_type=jnp.float32)


def norm_rows(value, gain):
    center = value - jnp.mean(value, axis=-1, keepdims=True)
    spread = jnp.mean(center * center, axis=-1, keepdims=True)
    return center * lax.rsqrt(spread + EPS) * gain


def norm_back(value, gain, grad):
    unused, pull = jax.vjp(norm_rows, value, gain.astype(jnp.float32))
    return pull(grad)


def gelu_back(value, grad):
    unused, pull = jax.vjp(jax.nn.gelu, value)
    return pull(grad)[0]


def split_heads(qkv_rows):
    parts = qkv_rows.reshape(qkv_rows.shape[0], 3, HEADS, HEAD_DIM)
    return (parts[:, 0], parts[:, 1], parts[:, 2])


def score_rows(queries, keys, items):
    raw = jnp.einsum(
        "qhd,khd->hqk", queries, keys, preferred_element_type=jnp.float32
    ) * HEAD_DIM ** (-0.5)
    places = jnp.arange(items.shape[0])
    allowed = (items[:, None] == items[None, :]) & (places[:, None] >= places[None, :])
    return jnp.where(allowed[None], raw, -jnp.inf)


def attend(qkv_rows, items):
    queries, keys, values = split_heads(qkv_rows)
    masked = score_rows(queries, keys, items)
    peak = jnp.max(masked, axis=-1, keepdims=True)
    log_total = peak + jnp.log(jnp.sum(jnp.exp(masked - peak), axis=-1, keepdims=True))
    probs = jnp.exp(masked - log_total).astype(LOW)
    mixed = jnp.einsum("hqk,khd->qhd", probs, values, preferred_element_type=jnp.float32)
    return (mixed.reshape(qkv_rows.shape[0], HEADS * HEAD_DIM).astype(LOW), log_total)


def attend_back(qkv_rows, items, log_total, grad_mixed):
    queries, keys, values = split_heads(qkv_rows)
    count = qkv_rows.shape[0]
    probs = jnp.exp(score_rows(queries, keys, items) - log_total)
    grad_heads = grad_mixed.reshape(count, HEADS, HEAD_DIM)
    grad_probs = jnp.einsum("qhd,khd->hqk", grad_heads, values, preferred_element_type=jnp.float32)
    delta = jnp.sum(probs * grad_probs, axis=-1, keepdims=True)
    grad_scores = (probs * (grad_probs - delta)).astype(LOW)
    scale = HEAD_DIM ** (-0.5)
    grad_q = (
        jnp.einsum("hqk,khd->qhd", grad_scores, keys, preferred_element_type=jnp.float32) * scale
    )
    grad_k = (
        jnp.einsum("hqk,qhd->khd", grad_scores, queries, preferred_element_type=jnp.float32) * scale
    )
    grad_v = jnp.einsum(
        "hqk,qhd->khd", probs.astype(LOW), grad_heads, preferred_element_type=jnp.float32
    )
    return (
        jnp.stack([grad_q, grad_k, grad_v], axis=1)
        .reshape(count, 3 * HEADS * HEAD_DIM)
        .astype(LOW)
    )


ROWS, COLS = 8, 4


class Links:
    def __init__(self, n_dp, n_fsdp):
        self.n, self.m = n_dp, n_fsdp
        self.near_n, self.near_m = n_dp // ROWS, n_fsdp // COLS
        self.d = lax.axis_index("dp")
        self.f = lax.axis_index("fsdp")
        self.row = self.d // self.near_n
        self.col = self.f // self.near_m
        self.spot = jnp.stack([self.row, self.col]).astype(jnp.int32)

    def swap(self, value, axis, bit):
        size = self.n if axis == "dp" else self.m
        return lax.ppermute(value, axis, [(i, i ^ bit) for i in range(size)])

    def across(self, value, step):
        axis, bit = step
        return self.swap(value, axis, bit * (self.near_n if axis == "dp" else self.near_m))

    def near_steps(self):
        steps = []
        for axis, size in (("fsdp", self.near_m), ("dp", self.near_n)):
            bit = 1
            while bit < size:
                steps.append((axis, bit))
                bit *= 2
        return steps

    def fill(self, piece):
        for axis, bit in self.near_steps():
            index, along = (self.d, 0) if axis == "dp" else (self.f, 1)
            other = self.swap(piece, axis, bit)
            piece = jnp.where(
                (index & bit) != 0,
                jnp.concatenate([other, piece], axis=along),
                jnp.concatenate([piece, other], axis=along),
            )
        return piece

    def drain(self, total):
        for axis, bit in reversed(self.near_steps()):
            index, along = (self.d, 0) if axis == "dp" else (self.f, 1)
            first, second = jnp.split(total, 2, axis=along)
            high = (index & bit) != 0
            give = jnp.where(high, first, second).astype(LOW)
            keep = jnp.where(high, second, first)
            total = keep + self.swap(give, axis, bit).astype(jnp.float32)
        return total

    def gather(self, piece, steps):
        group = piece[None]
        for step in steps[:3]:
            group = jnp.concatenate([group, self.across(group, step)])
        beside = self.across(group, steps[3])
        return (group, beside, self.across(group, steps[4]), self.across(beside, steps[4]))

    def scatter(self, parts, steps):
        here, beside, over, far = parts
        wide = jnp.float32

        def add(left, right):
            return (left.astype(wide) + right.astype(wide)).astype(LOW)

        beside = add(beside, self.across(far, steps[4]))
        got = self.across(over, steps[4])
        moved = self.across(beside, steps[3])
        terms = [here, got, moved]
        for step in reversed(steps[:3]):
            half = terms[0].shape[0] // 2
            give = sum(term[half:].astype(wide) for term in terms).astype(LOW)
            terms = [term[:half] for term in terms] + [self.across(give, step)]
        return sum(term[0].astype(wide) for term in terms)

    def gather_all(self, piece):
        steps = [("dp", 4), ("dp", 2), ("dp", 1), ("fsdp", 2), ("fsdp", 1)]
        group = piece[None]
        for axis, bit in steps:
            index = self.row if axis == "dp" else self.col
            other = self.across(group, (axis, bit))
            pair = jnp.where(
                (index & bit) != 0, jnp.stack([other, group]), jnp.stack([group, other])
            )
            group = pair.reshape((-1,) + piece.shape)
        group = group.reshape((2,) * 5 + piece.shape)
        return group.transpose(4, 3, 2, 1, 0, 5, 6).reshape((ROWS, COLS) + piece.shape)

    def scatter_all(self, total):
        steps = [("fsdp", 1), ("fsdp", 2), ("dp", 1), ("dp", 2), ("dp", 4)]
        group = total.reshape((2,) * 5 + total.shape[2:]).transpose(4, 3, 2, 1, 0, 5, 6)
        for axis, bit in steps:
            index = self.row if axis == "dp" else self.col
            high = (index & bit) != 0
            keep = jnp.where(high, group[1], group[0])
            give = jnp.where(high, group[0], group[1]).astype(LOW)
            group = keep + self.across(give, (axis, bit)).astype(jnp.float32)
        return group


FAR, NEAR, SIDE, BESIDE, CORE = ("dp", 4), ("dp", 2), ("dp", 1), ("fsdp", 2), ("fsdp", 1)
BY_COLUMNS = (FAR, SIDE, NEAR, BESIDE, CORE)
BY_ROWS = (FAR, BESIDE, NEAR, SIDE, CORE)


def places(steps):
    found = []
    for quarter in range(4):
        for index in range(8):
            row = col = 0
            for s, (axis, bit) in enumerate(steps):
                on = (index >> s) & 1 if s < 3 else (quarter >> (s - 3)) & 1
                if on and axis == "dp":
                    row |= bit
                elif on:
                    col |= bit
            found.append((quarter, index, row, col))
    return found


def plain(r, c):
    return [(0, (0, r), (0, c), (r, c, 0, False))]


def turned(r, c):
    return [(0, (0, r), (0, c), (r, c, 0, True))]


def stacked(r, c):
    return [
        (0, (0, r), (0, c), (r, c, 0, False)),
        (1, (r, r), (0, c // 2), (2 * r, c // 2, 0, True)),
        (1, (r, r), (c // 2, c // 2), (2 * r, c // 2, r, True)),
    ]


def copies(spot, quarters, wholes, layout, steps):
    row0, col0 = spot[0], spot[1]
    pairs = []
    for quarter, index, row, col in places(steps):
        row, col = row0 ^ row, col0 ^ col
        for which, (r, nr), (c, nc), (tall, broad, extra, swapped) in layout:
            down, right = (col, row) if swapped else (row, col)
            top = pl.multiple_of(down * tall + extra, 16)
            left = pl.multiple_of(right * broad, 128)
            pairs.append(
                (
                    quarters[quarter].at[index, pl.ds(r, nr), pl.ds(c, nc)],
                    wholes[which].at[pl.ds(top, nr), pl.ds(left, nc)],
                )
            )
    return pairs


def assemble(links, quarters, layout, steps, shapes):
    count = 32 * len(layout)

    def kernel(spot, a, b, c, d, *rest):
        wholes, sems = rest[:-1], rest[-1]
        moves = copies(spot, (a, b, c, d), wholes, layout, steps)
        moves = [pltpu.make_async_copy(s, t, sems.at[i]) for i, (s, t) in enumerate(moves)]
        for move in moves:
            move.start()
        for move in moves:
            move.wait()

    size = sum(h * w * 2 for h, w in shapes)
    return pl.pallas_call(
        kernel,
        out_shape=[jax.ShapeDtypeStruct(shape, LOW) for shape in shapes],
        in_specs=[pl.BlockSpec(memory_space=pltpu.SMEM)] + [pl.BlockSpec(memory_space=pl.ANY)] * 4,
        out_specs=[pl.BlockSpec(memory_space=pltpu.VMEM)] * len(shapes),
        scratch_shapes=[pltpu.SemaphoreType.DMA((count,))],
        compiler_params=pltpu.CompilerParams(vmem_limit_bytes=24 << 20),
        cost_estimate=pl.CostEstimate(flops=0, transcendentals=0, bytes_accessed=2 * size),
        name="assemble",
    )(links.spot, *quarters)


def take_apart(links, wholes, layout, steps, piece):
    count = 32 * len(layout)
    n = len(wholes)

    def kernel(spot, *rest):
        wholes, quarters, sems = rest[:n], rest[n : n + 4], rest[-1]
        moves = copies(spot, quarters, wholes, layout, steps)
        moves = [pltpu.make_async_copy(t, s, sems.at[i]) for i, (s, t) in enumerate(moves)]
        for move in reversed(moves):
            move.start()
        for move in moves:
            move.wait()

    size = sum(w.size * 2 for w in wholes)
    return pl.pallas_call(
        kernel,
        out_shape=[jax.ShapeDtypeStruct((8,) + piece, LOW)] * 4,
        in_specs=[pl.BlockSpec(memory_space=pltpu.SMEM)] + [pl.BlockSpec(memory_space=pltpu.VMEM)] * n,
        out_specs=[pl.BlockSpec(memory_space=pl.ANY)] * 4,
        scratch_shapes=[pltpu.SemaphoreType.DMA((count,))],
        compiler_params=pltpu.CompilerParams(vmem_limit_bytes=24 << 20),
        cost_estimate=pl.CostEstimate(flops=0, transcendentals=0, bytes_accessed=2 * size),
        name="take_apart",
    )(links.spot, *wholes)


def fold(shard):
    turned_shard = shard.T
    return jnp.concatenate(jnp.split(turned_shard, 2, axis=0), axis=1)


def unfold(piece):
    return jnp.concatenate(jnp.split(piece, 2, axis=1), axis=0).T


def per_device(
    n_dp,
    n_fsdp,
    byte_tokens,
    byte_mask,
    patch_item,
    cotangent,
    embed,
    patch_weight,
    gain_attn,
    qkv_weight,
    out_weight,
    gain_mlp,
    up_weight,
    down_weight,
    global_to_local,
    gain_local,
    local_up,
    local_down,
):
    links = Links(n_dp, n_fsdp)
    packed_gains = n_dp * n_fsdp == ROWS * COLS
    npatch, patch_len = byte_tokens.shape
    nbyte = npatch * patch_len

    def shard(weight):
        return links.fill(weight.astype(LOW))

    s_embed, s_patch, s_qkv, s_out = map(shard, (embed, patch_weight, qkv_weight, out_weight))
    s_up, s_down, s_link = map(shard, (up_weight, down_weight, global_to_local))
    s_local_up, s_local_down = map(shard, (local_up, local_down))
    r_embed, c_embed = s_embed.shape
    vocab, width = r_embed * ROWS, c_embed * COLS
    r, c_qkv = s_qkv.shape
    c_out, c_up, c_link = s_out.shape[1], s_up.shape[1], s_link.shape[1]
    c_att = c_qkv + c_out
    hidden = c_up * COLS

    gains = jnp.stack([gain_attn, gain_mlp, gain_local]).astype(LOW)
    per_gain = gains.shape[1]
    if packed_gains:
        gain_row = jnp.pad(gains.reshape(1, -1), ((0, 15), (0, c_embed - 3 * per_gain)))
        everyone = links.gather_all(jnp.concatenate([s_embed, gain_row]))
        all_gains = everyone[:, :, r_embed, : 3 * per_gain].reshape(-1, 3, per_gain)
        all_gains = all_gains.transpose(1, 0, 2).reshape(3, width)
    else:
        everyone = links.gather_all(s_embed)
        all_gains = lax.all_gather(gains, ("dp", "fsdp"), axis=1, tiled=True)
    w_embed = everyone[:, :, :r_embed].transpose(0, 2, 1, 3).reshape(vocab, width)
    g_attn, g_mlp, g_local = all_gains.astype(jnp.float32)

    table = lax.dot_general(
        s_patch, w_embed, (((0,), (1,)), ((), ())), preferred_element_type=jnp.float32
    ).astype(LOW)

    att_piece = jnp.concatenate([s_qkv, s_out], axis=1)
    mlp_piece = jnp.concatenate([s_up, fold(s_down)])
    local_piece = jnp.concatenate([s_local_up, fold(s_local_down)])
    att_layout, mlp_layout = plain(r, c_att), stacked(r, c_up)
    link_layout, table_layout = plain(r, c_link), turned(c_embed, vocab)

    def whole(piece, layout, steps, shapes):
        return assemble(links, links.gather(piece, steps), layout, steps, shapes)

    (w_att,) = whole(att_piece, att_layout, BY_ROWS, [(width, COLS * c_att)])
    (w_table,) = whole(table, table_layout, BY_ROWS, [(width, ROWS * vocab)])
    w_up, w_down = whole(mlp_piece, mlp_layout, BY_COLUMNS, [(width, hidden)] * 2)
    (w_link,) = whole(s_link, link_layout, BY_ROWS, [(width, COLS * c_link)])
    w_local_up, w_local_down = whole(local_piece, mlp_layout, BY_COLUMNS, [(width, hidden)] * 2)

    def summed(wholes, layout, steps, piece):
        wholes = [total.astype(LOW) for total in wholes]
        return links.scatter(take_apart(links, wholes, layout, steps, piece), steps)

    byte_live = byte_mask.reshape(-1).astype(jnp.float32)[:, None]
    marked = jnp.where(byte_mask != 0, byte_tokens, -1)
    before = jnp.concatenate([jnp.full((npatch, 1), -1, jnp.int32), marked[:, :-1]], axis=1)
    values = jnp.arange(vocab, dtype=jnp.int32)
    hot_before = (before.reshape(-1)[:, None] == values[None, :]).astype(LOW)
    hot_patch = jnp.concatenate(
        [(marked[:, k : k + 1] == values[None, :]).astype(LOW) for k in range(patch_len)], axis=1
    )
    grad_out = cotangent.astype(jnp.float32) * byte_live
    grad_lout = grad_out.astype(LOW)

    patch_emb = times_back(hot_patch, w_table)
    same_item = (patch_item[1:] == patch_item[:-1]).astype(jnp.float32)[:, None]
    global_in = jnp.concatenate(
        [jnp.zeros((1, width), jnp.float32), patch_emb[:-1] * same_item], axis=0
    )
    normed_attn = norm_rows(global_in, g_attn).astype(LOW)
    att_rows = matmul(normed_attn, w_att).astype(LOW)
    blocks = [att_rows[:, i * c_att : i * c_att + c_qkv] for i in range(COLS)]
    qkv_rows = jnp.concatenate(blocks, axis=1)
    mixed, log_total = attend(qkv_rows, patch_item)
    out_rows = matmul(mixed, w_att)
    blocks = [out_rows[:, i * c_att + c_qkv : (i + 1) * c_att] for i in range(COLS)]
    after_attn = global_in + jnp.concatenate(blocks, axis=1)
    normed_mlp = norm_rows(after_attn, g_mlp).astype(LOW)
    hidden_pre = matmul(normed_mlp, w_up)
    hidden_act = jax.nn.gelu(hidden_pre).astype(LOW)
    global_out = after_attn + times_back(hidden_act, w_down)
    global_low = global_out.astype(LOW)
    from_global = matmul(global_low, w_link).reshape(nbyte, width)
    local_in = from_global + matmul(hot_before, w_embed)
    normed_local = norm_rows(local_in, g_local).astype(LOW)
    local_pre = matmul(normed_local, w_local_up)
    local_act = jax.nn.gelu(local_pre).astype(LOW)
    local_out = local_in + times_back(local_act, w_local_down)
    result = (local_out * byte_live).astype(LOW)

    local_down_total = over_rows(grad_lout, local_act)
    grad_local_act = matmul(grad_lout, w_local_down)
    grad_local_pre = gelu_back(local_pre, grad_local_act).astype(LOW)
    local_up_total = over_rows(normed_local, grad_local_pre)
    local_sum = summed((local_up_total, local_down_total), mlp_layout, BY_COLUMNS, local_piece.shape)
    grad_normed_local = times_back(grad_local_pre, w_local_up)
    grad_local_in, grad_gain_local = norm_back(local_in, g_local, grad_normed_local)
    grad_local_in = grad_local_in + grad_out
    grad_local_low = grad_local_in.astype(LOW)
    grad_link_in = grad_local_low.reshape(npatch, patch_len * width)
    link_sum = summed((over_rows(global_low, grad_link_in),), link_layout, BY_ROWS, s_link.shape)
    grad_global_out = times_back(grad_link_in, w_link)
    embed_direct = over_rows(hot_before, grad_local_low)

    grad_mlp = grad_global_out.astype(LOW)
    down_total = over_rows(grad_mlp, hidden_act)
    grad_hidden = matmul(grad_mlp, w_down)
    grad_hidden_pre = gelu_back(hidden_pre, grad_hidden).astype(LOW)
    up_total = over_rows(normed_mlp, grad_hidden_pre)
    mlp_sum = summed((up_total, down_total), mlp_layout, BY_COLUMNS, mlp_piece.shape)
    grad_normed_mlp = times_back(grad_hidden_pre, w_up)
    grad_after, grad_gain_mlp = norm_back(after_attn, g_mlp, grad_normed_mlp)
    grad_after = grad_after + grad_global_out
    grad_attn = grad_after.astype(LOW)

    def spread(value, start):
        w = value.shape[1] // COLS
        edges = ((0, 0), (start, c_att - start - w))
        parts = [jnp.pad(value[:, i * w : (i + 1) * w], edges) for i in range(COLS)]
        return jnp.concatenate(parts, axis=1)

    out_side = spread(grad_attn, c_qkv)
    grad_mixed = times_back(out_side, w_att).astype(LOW)
    qkv_side = spread(attend_back(qkv_rows, patch_item, log_total, grad_mixed), 0)
    att_total = over_rows(
        jnp.concatenate([normed_attn, mixed]), jnp.concatenate([qkv_side, out_side])
    )
    att_sum = summed((att_total,), att_layout, BY_ROWS, att_piece.shape)
    grad_normed_attn = times_back(qkv_side, w_att)
    grad_global_in, grad_gain_attn = norm_back(global_in, g_attn, grad_normed_attn)
    grad_global_in = grad_global_in + grad_after
    grad_patch_emb = jnp.concatenate(
        [grad_global_in[1:] * same_item, jnp.zeros((1, width), jnp.float32)], axis=0
    ).astype(LOW)
    table_total = over_rows(grad_patch_emb, hot_patch)
    table_grad = summed((table_total,), table_layout, BY_ROWS, table.shape).astype(LOW)
    patch_grad = lax.dot_general(
        w_embed, table_grad, (((0,), (1,)), ((), ())), preferred_element_type=jnp.float32
    )
    embed_partial = embed_direct + lax.dot_general(
        table_grad, s_patch, (((0,), (1,)), ((), ())), preferred_element_type=jnp.float32
    )
    embed_partial = embed_partial.reshape(ROWS, r_embed, COLS, c_embed).transpose(0, 2, 1, 3)
    gain_grads = jnp.stack([grad_gain_attn, grad_gain_mlp, grad_gain_local])
    if packed_gains:
        gain_rows = gain_grads.reshape(3, ROWS, COLS, per_gain).transpose(1, 2, 0, 3)
        gain_rows = gain_rows.reshape(ROWS, COLS, 1, 3 * per_gain)
        gain_rows = jnp.pad(gain_rows, ((0, 0), (0, 0), (0, 15), (0, c_embed - 3 * per_gain)))
        sums = links.scatter_all(jnp.concatenate([embed_partial, gain_rows], axis=2))
        gain_sums = sums[r_embed, : 3 * per_gain].reshape(3, per_gain)
    else:
        sums = links.scatter_all(embed_partial)
        gain_sums = lax.psum_scatter(
            gain_grads.astype(LOW), ("dp", "fsdp"), scatter_dimension=1, tiled=True
        ).astype(jnp.float32)
    drain = links.drain
    return (
        result,
        drain(sums[:r_embed]),
        drain(patch_grad),
        gain_sums[0],
        drain(att_sum[:, :c_qkv]),
        drain(att_sum[:, c_qkv:]),
        gain_sums[1],
        drain(mlp_sum[:r]),
        drain(unfold(mlp_sum[r:])),
        drain(link_sum),
        gain_sums[2],
        drain(local_sum[:r]),
        drain(unfold(local_sum[r:])),
    )


def solution(mesh):
    n_dp, n_fsdp = mesh.shape["dp"], mesh.shape["fsdp"]

    def body(*args):
        return per_device(n_dp, n_fsdp, *args)

    items = P(("dp", "fsdp"), None)
    weight = P("dp", "fsdp")
    flat = P(("dp", "fsdp"))
    weights = (weight, weight, flat, weight, weight, flat, weight, weight, weight, flat, weight, weight)
    return jax.shard_map(
        body,
        mesh=mesh,
        in_specs=(items, items, flat, items) + weights,
        out_specs=(items,) + weights,
        check_vma=False,
    )
```
